512 devices in a mesh: leaf: 16 (over z), col: 32 (over y, x, core).
Axes of the slice: x: 4, y: 4, z: 16, core: 2. Of those that a mesh axis runs over, the one named last changes fastest.
Arguments:
- leaf_solution: float32 [16, 16384, 256], P('leaf', 'col'), may hold values from -6 to 6
- coupling: float32 [16, 768, 128, 128], P('leaf', 'col'), may hold values from -0.01953125 to 0.01953125
- tile_slot: int32 [16, 768], P('leaf', 'col'), may hold values from 0 to 63, as said below
- sep_rhs: float32 [2048, 256], P('col'), may hold values from -6 to 6
- pivot_inverse: float32 [16, 128, 128], P('leaf'), as said below
Outputs:
- sep_solution: float32 [2048, 256], P('col')
- leaf_update: float32 [16, 16384, 256], P('leaf', 'col')
The draws below stay inside these ranges and needn't reach their ends.
Inputs may be any that keep to these rules, and one draw needn't show every extreme that they name: `tile_slot`: within each aligned block of 24 entries along dimension 1 the values are distinct. `pivot_inverse`: each block is symmetric.
All inputs are finite; a program needn't handle non-finite values.
Results may differ from the reference program's by a relative error of at most 0.0003.
Values sent between devices are 32-bit elements; how exact they have to be, the bound alone decides.
No kernel may reach another device: no remote copies, remote signals or barrier semaphores. Data moves between devices by JAX's collectives and lax.ppermute only.
A program may use at most 64 MiB of HBM per device.

```python
import jax
import jax.numpy as jnp
from jax import lax

SEP = 2048
NRHS = 256
BLOCK = 128
LEAF_DEV = 512
TILES = 24
N_LEAF = 16
N_COL = 32


def draw_tile_slot(key, part):
    slot_total = SEP // BLOCK * (LEAF_DEV // BLOCK)
    keys = jax.random.split(jax.random.fold_in(key, 11), N_LEAF * N_COL)

    def pick(one_key):
        return jax.random.permutation(one_key, jnp.arange(slot_total, dtype=jnp.int32))[:TILES]
    chosen = jax.vmap(pick)(keys)
    return chosen.reshape(N_LEAF, N_COL * TILES).astype(jnp.int32)


def draw_pivot_inverse(key, part):
    key_off = jax.random.fold_in(key, 21)
    key_diag = jax.random.fold_in(key, 22)
    count = SEP // BLOCK
    off = jax.random.normal(key_off, (count, BLOCK, BLOCK), jnp.float32) * 0.15
    off = (off + jnp.swapaxes(off, 1, 2)) * 0.7071
    diag = jax.random.uniform(key_diag, (count, BLOCK), jnp.float32, 1.0, 4.0)
    eye = jnp.eye(BLOCK, dtype=jnp.float32)
    return off * (1.0 - eye) + eye * diag[:, :, None]


def levels(own_key, extent, pieces, smallest, top_value):
    def one(axis_at, blocks):
        steps = jax.random.uniform(jax.random.fold_in(jax.random.fold_in(own_key, 6), axis_at), (blocks,), jnp.float32, smallest / len(pieces), top_value / len(pieces))
        return jnp.repeat(jnp.exp(steps), extent[axis_at] // blocks).reshape((-1,) + (1,) * (len(extent) - axis_at - 1))

    level = one(*pieces[0])
    for cut in pieces[1:]:
        level = level * one(*cut)
    return level


def normal_values(key, extent, scale, bound, shards=(), held_as=jnp.bfloat16):
    gain = levels(key, extent, shards, -0.22, 0.18) if shards else 1.0
    array = jax.random.normal(key, extent, jnp.float32) * scale * gain
    return jnp.minimum(jnp.maximum(array, -bound), bound).astype(held_as)


def setup_inputs(seed: int = 0) -> dict:
    key_of = jax.random.split(jax.random.key(seed), 6)
    leaf_solution = normal_values(key_of[0], (N_LEAF, N_COL * LEAF_DEV, NRHS), 1.0, 6.0, ((0, 16), (1, 32)), jnp.float32)
    coupling = normal_values(key_of[1], (N_LEAF, N_COL * TILES, BLOCK, BLOCK), (N_LEAF * N_COL * TILES * BLOCK * BLOCK // SEP) ** -0.5, 0.01953125, ((0, 16), (1, 32)), jnp.float32)
    tile_slot = draw_tile_slot(jax.random.fold_in(key_of[5], 71), 0)
    sep_rhs = normal_values(key_of[3], (SEP, NRHS), 1.0, 6.0, ((0, 32),), jnp.float32)
    pivot_inverse = draw_pivot_inverse(jax.random.fold_in(key_of[5], 71), 0)
    return {"leaf_solution": leaf_solution, "coupling": coupling, "tile_slot": tile_slot, "sep_rhs": sep_rhs, "pivot_inverse": pivot_inverse}


def reference(leaf_solution, coupling, tile_slot, sep_rhs, pivot_inverse):
    precise = lax.Precision.HIGHEST
    row_blocks = SEP // BLOCK
    col_blocks = LEAF_DEV // BLOCK
    devices_all = N_LEAF * N_COL
    leaf_blocks = leaf_solution.reshape(devices_all, col_blocks, BLOCK, NRHS)
    tile_data = coupling.reshape(devices_all, TILES, BLOCK, BLOCK)
    slot_ids = tile_slot.reshape(devices_all, TILES).astype(jnp.int32)

    def forward(carry, items):
        blocks_here, tiles_here, slots_here = items
        tile_row = slots_here // col_blocks
        tile_col = slots_here % col_blocks
        picked = blocks_here[tile_col]
        products = jnp.einsum("tij,tjk->tik", tiles_here, picked, precision=precise)
        summed = jax.ops.segment_sum(products, tile_row, num_segments=row_blocks)
        return carry + summed, None

    start = jnp.zeros((row_blocks, BLOCK, NRHS), jnp.float32)
    coupled, _ = lax.scan(forward, start, (leaf_blocks, tile_data, slot_ids))
    reduced = sep_rhs - coupled.reshape(SEP, NRHS)
    solution = jnp.einsum("bij,bjk->bik", pivot_inverse, reduced.reshape(row_blocks, BLOCK, NRHS), precision=precise)

    def backward(items):
        blocks_here, tiles_here, slots_here = items
        tile_row = slots_here // col_blocks
        tile_col = slots_here % col_blocks
        chosen = solution[tile_row]
        transposed = jnp.einsum("tij,tik->tjk", tiles_here, chosen, precision=precise)
        update = jax.ops.segment_sum(transposed, tile_col, num_segments=col_blocks)
        return blocks_here - update

    updated = lax.map(backward, (leaf_blocks, tile_data, slot_ids))
    return solution.reshape(SEP, NRHS), updated.reshape(N_LEAF, N_COL * LEAF_DEV, NRHS)
```

```python
import jax
import jax.numpy as jnp
from jax import lax
from jax.experimental import pallas as pl
from jax.experimental.pallas import tpu as pltpu
from jax.sharding import Mesh, PartitionSpec as P

F32 = jnp.float32
BF16 = jnp.bfloat16


def split(value):
    high = value.astype(BF16)
    low = (value - high.astype(F32)).astype(BF16)
    return high, low


def forward_kernel(info, slots, leaf, tiles, rhs, own, send, lhs):
    z, chip, core = info[0], info[1], info[2]
    count, size = tiles.shape[0], tiles.shape[1]
    col_blocks = leaf.shape[0] // size
    slabs = own.shape[0]
    halves = ((own, pl.multiple_of(core * size, size)), (send, pl.multiple_of((1 - core) * size, size)))
    lane = lax.broadcasted_iota(jnp.int32, (size, size), 1)
    keep = (lane // (size // 2) == core) & (z == 0)
    for part, (out, start) in enumerate(halves):
        out[...] = jnp.zeros_like(out)
        piece = rhs[:, pl.ds(start, size)]
        placed = jnp.where(keep, jnp.concatenate([piece, piece], 0).T, 0.0)
        out[:, chip] = placed.reshape(slabs, 8, size)
        for b in range(col_blocks):
            high, low = split(leaf[b * size : (b + 1) * size, pl.ds(start, size)].T)
            lhs[b, part * size : (part + 1) * size] = jnp.concatenate([high, high, low], 1)

    def product(t):
        high, low = split(tiles[t])
        weights = jnp.concatenate([high, low, high], 1)
        return lax.dot_general(
            lhs[slots[t] % col_blocks], weights, (((1,), (1,)), ((), ())), preferred_element_type=F32
        )

    def add(t, value):
        row = slots[t] // col_blocks
        own[:, row] -= value[:size].reshape(slabs, 8, size)
        send[:, row] -= value[size:].reshape(slabs, 8, size)

    ahead = product(0)
    for t in range(count):
        value = ahead
        if t + 1 < count:
            ahead = product(t + 1)
        add(t, value)


def solve_kernel(parts, pivot, out):
    total = jnp.sum(parts[...], 0)
    solved = jnp.dot(total, pivot[0], preferred_element_type=F32, precision=lax.Precision.HIGHEST)
    out[...] = jnp.broadcast_to(solved[None], out.shape)


def backward_kernel(info, slots, leaf, tiles, own, other, sep_out, leaf_out, lhs, update, turned):
    chip, core = info[1], info[2]
    count, size = tiles.shape[0], tiles.shape[1]
    col_blocks = leaf.shape[0] // size
    row_blocks = own.shape[1]
    halves = ((own, pl.multiple_of(core * size, size)), (other, pl.multiple_of((1 - core) * size, size)))
    update[...] = jnp.zeros_like(update)
    for part, (ref, start) in enumerate(halves):
        turned[:, pl.ds(start, size)] = ref[:, chip].reshape(size, size).T
        for k in range(row_blocks):
            high, low = split(ref[:, k].reshape(size, size))
            lhs[k, part * size : (part + 1) * size] = jnp.concatenate([high, high, low], 1)
    rows = sep_out.shape[0]
    sep_out[...] = turned[pl.ds(pl.multiple_of(core * rows, rows), rows), :]

    def product(t):
        high, low = split(tiles[t])
        weights = jnp.concatenate([high, low, high], 0)
        return jnp.dot(lhs[slots[t] // col_blocks], weights, preferred_element_type=F32)

    ahead = product(0)
    for t in range(count):
        value = ahead
        if t + 1 < count:
            ahead = product(t + 1)
        update[slots[t] % col_blocks] += value
    for b in range(col_blocks):
        rows_b = slice(b * size, (b + 1) * size)
        for part, (_, start) in enumerate(halves):
            change = update[b, part * size : (part + 1) * size].T
            leaf_out[rows_b, pl.ds(start, size)] = leaf[rows_b, pl.ds(start, size)] - change


def on_device(leaf_solution, coupling, tile_slot, sep_rhs, pivot_inverse):
    n_z, n_x = lax.axis_size("z"), lax.axis_size("x")
    n_chip = lax.axis_size("y") * n_x
    leaf, tiles, slots = leaf_solution[0], coupling[0], tile_slot[0]
    size = tiles.shape[-1]
    count = tiles.shape[0]
    row_blocks = n_z
    col_blocks = leaf.shape[0] // size
    rhs_count = leaf.shape[1]
    core = lax.axis_index("c")
    info = jnp.stack([lax.axis_index("z"), lax.axis_index("y") * n_x + lax.axis_index("x"), core]).astype(jnp.int32)
    smem = pl.BlockSpec(memory_space=pltpu.SMEM)
    vmem = pl.BlockSpec(memory_space=pltpu.VMEM)
    part = jax.ShapeDtypeStruct((n_chip, row_blocks, 8, size), F32)
    own, send = pl.pallas_call(
        forward_kernel,
        out_shape=(part, part),
        in_specs=[smem, smem, vmem, vmem, vmem],
        out_specs=(vmem, vmem),
        scratch_shapes=[pltpu.VMEM((col_blocks, rhs_count, 3 * size), BF16)],
        name="forward",
    )(info, slots, leaf, tiles, sep_rhs)
    swap = [(0, 1), (1, 0)]
    half = own + lax.ppermute(send, "c", swap)
    shared = lax.all_to_all(half, ("y", "x"), 0, 0, tiled=True)
    slab = jnp.sum(shared, 0)
    parts = lax.all_to_all(slab, "z", 0, 0, tiled=True)
    copies = pl.pallas_call(
        solve_kernel,
        out_shape=jax.ShapeDtypeStruct(parts.shape, F32),
        in_specs=[vmem, vmem],
        out_specs=vmem,
        name="solve",
    )(parts, pivot_inverse)
    blocks = lax.all_to_all(copies, "z", 0, 0, tiled=True)
    wide = jnp.broadcast_to(blocks[None], (n_chip,) + blocks.shape)
    mine = lax.all_to_all(wide, ("y", "x"), 0, 0, tiled=True)
    other = lax.ppermute(mine, "c", swap)
    sep_solution, leaf_update = pl.pallas_call(
        backward_kernel,
        out_shape=(jax.ShapeDtypeStruct(sep_rhs.shape, F32), jax.ShapeDtypeStruct(leaf.shape, F32)),
        in_specs=[smem, smem, vmem, vmem, vmem, vmem],
        out_specs=(vmem, vmem),
        scratch_shapes=[
            pltpu.VMEM((row_blocks, rhs_count, 3 * size), BF16),
            pltpu.VMEM((col_blocks, rhs_count, size), F32),
            pltpu.VMEM((size, rhs_count), F32),
        ],
        name="backward",
    )(info, slots, leaf, tiles, mine, other)
    return sep_solution, leaf_update[None]


def solution(mesh):
    chips = mesh.devices.reshape(mesh.shape["leaf"], 4, mesh.shape["col"] // 8, 2)
    fine = Mesh(chips, ("z", "y", "x", "c"))
    col = ("y", "x", "c")
    return jax.shard_map(
        on_device,
        mesh=fine,
        in_specs=(P("z", col, None), P("z", col, None, None), P("z", col), P(col, None), P("z", None, None)),
        out_specs=(P(col, None), P("z", col, None)),
        check_vma=False,
    )
```

```python
from functools import partial

import jax
import jax.numpy as jnp
from jax import lax
from jax.experimental import pallas as pl
from jax.experimental.pallas import tpu as pltpu
from jax.sharding import Mesh, PartitionSpec as P

F32 = jnp.float32
BF16 = jnp.bfloat16


def split(value):
    high = value.astype(BF16)
    low = (value - high.astype(F32)).astype(BF16)
    return high, low


def place():
    return lax.axis_index("z"), lax.axis_index("y") * lax.axis_size("x") + lax.axis_index("x"), lax.axis_index("c")


def half_start(core, size):
    return pl.multiple_of(core * size, size)


def chunk_copies(source, target, sems):
    step = source.shape[0] // sems.shape[0]
    chunks = [pl.ds(i * step, step) for i in range(sems.shape[0])]
    copies = [pltpu.make_async_copy(source.at[c], target.at[c], sems.at[i]) for i, c in enumerate(chunks)]
    for copy in copies:
        copy.start()
    return copies


def pipelined(copies, count, product, use):
    step = count // len(copies)
    ahead = None
    for t in range(count + 1):
        value = ahead
        if t < count:
            if t % step == 0:
                copies[t // step].wait()
            ahead = product(t)
        if t > 0:
            use(t - 1, value)


def forward_kernel(swapped, slots, leaf, tiles_hbm, rhs, out, lhs, tiles, sems):
    copies = chunk_copies(tiles_hbm, tiles, sems)
    z, chip, core = place()
    count, size = tiles.shape[0], tiles.shape[1]
    col_blocks = leaf.shape[0] // size
    slabs = out.shape[0]
    start = half_start(1 - core if swapped else core, size)
    lane = lax.broadcasted_iota(jnp.int32, (size, size), 1)
    keep = (lane // (size // 2) == core) & (z == 0)
    out[...] = jnp.zeros_like(out)
    piece = rhs[:, pl.ds(start, size)]
    placed = jnp.where(keep, jnp.concatenate([piece, piece], 0).T, 0.0)
    out[:, chip] = placed.reshape(slabs, 8, size)
    for b in range(col_blocks):
        high, low = split(leaf[b * size : (b + 1) * size, pl.ds(start, size)].T)
        lhs[b] = jnp.concatenate([high, high, low], 1)

    def product(t):
        high, low = split(tiles[t])
        weights = jnp.concatenate([high, low, high], 1)
        return lax.dot_general(
            lhs[slots[t] % col_blocks], weights, (((1,), (1,)), ((), ())), preferred_element_type=F32
        )

    def use(t, value):
        out[:, slots[t] // col_blocks] -= value.reshape(slabs, 8, size)

    pipelined(copies, count, product, use)


def solve_kernel(parts, pivot, out):
    total = jnp.sum(parts[...], 0)
    solved = jnp.dot(total, pivot[0], preferred_element_type=F32, precision=lax.Precision.HIGHEST)
    out[...] = jnp.broadcast_to(solved[None], out.shape)


def backward_half(swapped, slots, leaf_hbm, tiles_hbm, sol, to, sep_out, leaf_out, lhs, update, tiles, sems, leaf, leaf_sem):
    copies = chunk_copies(tiles_hbm, tiles, sems)
    leaf_copy = pltpu.make_async_copy(leaf_hbm, leaf, leaf_sem)
    leaf_copy.start()
    _, chip, core = place()
    count, size = tiles.shape[0], tiles.shape[1]
    col_blocks = leaf.shape[0] // size
    row_blocks = sol.shape[1]
    cols = pl.ds(half_start(1 - core if swapped else core, size), size)
    update[...] = jnp.zeros_like(update)
    for k in range(row_blocks):
        high, low = split(sol[:, k].reshape(size, size))
        lhs[k] = jnp.concatenate([high, high, low], 1)
    rows = sep_out.shape[0]
    turned = sol[:, chip].reshape(size, size).T
    to = cols if to is None else to
    sep_out[:, to] = jnp.where(core == 0, turned[:rows], turned[rows:])

    def product(t):
        high, low = split(tiles[t])
        weights = jnp.concatenate([high, low, high], 0)
        return jnp.dot(lhs[slots[t] // col_blocks], weights, preferred_element_type=F32)

    def use(t, value):
        update[slots[t] % col_blocks] += value

    pipelined(copies, count, product, use)
    leaf_copy.wait()
    for b in range(col_blocks):
        rows_b = slice(b * size, (b + 1) * size)
        leaf_out[rows_b, to] = leaf[rows_b, cols] - update[b].T


def backward_own(slots, leaf, tiles, sol, *rest):
    backward_half(False, slots, leaf, tiles, sol, slice(None), *rest)


def backward_other(slots, leaf, tiles, sol, sep_part, leaf_part, sep_out, leaf_out, *rest):
    size = tiles.shape[1]
    cols = pl.ds(half_start(place()[2], size), size)
    sep_out[:, cols] = sep_part[...]
    leaf_out[:, cols] = leaf_part[...]
    backward_half(True, slots, leaf, tiles, sol, None, sep_out, leaf_out, *rest)


def in_vmem(array):
    return pltpu.with_memory_space_constraint(array, pltpu.VMEM)


def on_device(leaf_solution, coupling, tile_slot, sep_rhs, pivot_inverse):
    n_z = lax.axis_size("z")
    n_chip = lax.axis_size("y") * lax.axis_size("x")
    slots = tile_slot[0]
    leaf, tiles, rhs, pivot = leaf_solution[0], coupling[0], sep_rhs, in_vmem(pivot_inverse)
    size = tiles.shape[-1]
    col_blocks = leaf.shape[0] // size
    smem = pl.BlockSpec(memory_space=pltpu.SMEM)
    vmem = pl.BlockSpec(memory_space=pltpu.VMEM)
    hbm = pl.BlockSpec(memory_space=pl.ANY)
    staging = [pltpu.VMEM(tiles.shape, F32), pltpu.SemaphoreType.DMA((4,))]

    def forward(swapped):
        return pl.pallas_call(
            partial(forward_kernel, swapped),
            out_shape=pltpu.VMEM((n_chip, n_z, 8, size), F32),
            in_specs=[smem, vmem, hbm, vmem],
            out_specs=vmem,
            scratch_shapes=[pltpu.VMEM((col_blocks, size, 3 * size), BF16)] + staging,
            name="forward_send" if swapped else "forward_own",
        )(slots, leaf, tiles, rhs)

    swap = [(0, 1), (1, 0)]
    arrived = lax.ppermute(forward(True), "c", swap)
    half = forward(False) + arrived
    shared = lax.all_to_all(half, ("y", "x"), 0, 0, tiled=True)
    slab = jnp.sum(shared, 0)
    parts = lax.all_to_all(slab, "z", 0, 0, tiled=True)
    copies = pl.pallas_call(
        solve_kernel,
        out_shape=pltpu.VMEM(parts.shape, F32),
        in_specs=[vmem, vmem],
        out_specs=vmem,
        name="solve",
    )(in_vmem(parts), pivot)
    blocks = lax.all_to_all(copies, "z", 0, 0, tiled=True)
    wide = jnp.broadcast_to(blocks[None], (n_chip,) + blocks.shape)
    mine = lax.all_to_all(wide, ("y", "x"), 0, 0, tiled=True)
    other = lax.ppermute(mine, "c", swap)
    scratch = [pltpu.VMEM((n_z, size, 3 * size), BF16), pltpu.VMEM((col_blocks, size, size), F32)]
    scratch += staging + [pltpu.VMEM(leaf.shape, F32), pltpu.SemaphoreType.DMA]
    parts_own = pl.pallas_call(
        backward_own,
        out_shape=(pltpu.VMEM((rhs.shape[0], size), F32), pltpu.VMEM((leaf.shape[0], size), F32)),
        in_specs=[smem, hbm, hbm, vmem],
        out_specs=(vmem, vmem),
        scratch_shapes=scratch,
        name="backward_own",
    )(slots, leaf, tiles, in_vmem(mine))
    sep_solution, leaf_update = pl.pallas_call(
        backward_other,
        out_shape=(jax.ShapeDtypeStruct(rhs.shape, F32), jax.ShapeDtypeStruct(leaf.shape, F32)),
        in_specs=[smem, hbm, hbm, vmem, vmem, vmem],
        out_specs=(vmem, vmem),
        scratch_shapes=scratch,
        name="backward_other",
    )(slots, leaf, tiles, in_vmem(other), *map(in_vmem, parts_own))
    return sep_solution, leaf_update[None]


def solution(mesh):
    chips = mesh.devices.reshape(mesh.shape["leaf"], 4, mesh.shape["col"] // 8, 2)
    fine = Mesh(chips, ("z", "y", "x", "c"))
    col = ("y", "x", "c")
    return jax.shard_map(
        on_device,
        mesh=fine,
        in_specs=(P("z", col, None), P("z", col, None, None), P("z", col), P(col, None), P("z", None, None)),
        out_specs=(P(col, None), P("z", col, None)),
        check_vma=False,
    )
```

```python
from functools import partial

import jax
import jax.numpy as jnp
from jax import lax
from jax.experimental import pallas as pl
from jax.experimental.pallas import tpu as pltpu
from jax.sharding import Mesh, PartitionSpec as P

F32 = jnp.float32
BF16 = jnp.bfloat16
CHUNKS = (8, 16)


def split(value):
    high = value.astype(BF16)
    low = (value - high.astype(F32)).astype(BF16)
    return high, low


def place():
    return lax.axis_index("z"), lax.axis_index("y") * lax.axis_size("x") + lax.axis_index("x"), lax.axis_index("c")


def half_columns(core, size):
    return pl.ds(pl.multiple_of(core * size, size), size)


def start_copies(pairs, tiles_hbm, tiles, sems):
    parts = [pl.ds(sum(CHUNKS[:i]), step) for i, step in enumerate(CHUNKS)]
    pairs = pairs + [(tiles_hbm.at[part], tiles.at[part]) for part in parts]
    copies = [pltpu.make_async_copy(source, target, sems.at[i]) for i, (source, target) in enumerate(pairs)]
    for copy in copies:
        copy.start()
    return copies[: -len(CHUNKS)], copies[-len(CHUNKS) :]


def pipelined(copies, count, product, use):
    first = {sum(CHUNKS[:i]): copy for i, copy in enumerate(copies)}
    ahead = None
    for t in range(count + 1):
        value = ahead
        if t < count:
            if t in first:
                first[t].wait()
            ahead = product(t)
        if t > 0:
            use(t - 1, value)


def forward_kernel(swapped, slots_hbm, leaf_hbm, tiles_hbm, rhs_hbm, out, lhs, tiles, slots, leaf, rhs, sems):
    z, chip, core = place()
    count, size = tiles.shape[0], tiles.shape[1]
    col_blocks = leaf.shape[0] // size
    slabs = out.shape[0]
    cols = half_columns(1 - core if swapped else core, size)
    small, copies = start_copies(
        [(leaf_hbm.at[:, cols], leaf), (slots_hbm, slots), (rhs_hbm.at[:, cols], rhs)], tiles_hbm, tiles, sems
    )
    out[...] = jnp.zeros_like(out)
    small[0].wait()
    for b in range(col_blocks):
        high, low = split(leaf[b * size : (b + 1) * size].T)
        lhs[b] = jnp.concatenate([high, high, low], 1)
    small[1].wait()
    small[2].wait()
    lane = lax.broadcasted_iota(jnp.int32, (size, size), 1)
    keep = (lane // (size // 2) == core) & (z == 0)
    placed = jnp.where(keep, jnp.concatenate([rhs[...], rhs[...]], 0).T, 0.0)
    out[:, chip] = placed.reshape(slabs, 8, size)

    def product(t):
        high, low = split(tiles[t])
        weights = jnp.concatenate([high.T, low.T, high.T], 0)
        return jnp.dot(lhs[slots[t] % col_blocks], weights, preferred_element_type=F32)

    def use(t, value):
        out[:, slots[t] // col_blocks] -= value.reshape(slabs, 8, size)

    pipelined(copies, count, product, use)


def solve_kernel(parts, pivot, out):
    total = jnp.sum(parts[...], 0)
    solved = jnp.dot(total, pivot[0], preferred_element_type=F32, precision=lax.Precision.HIGHEST)
    out[...] = jnp.broadcast_to(solved[None], out.shape)


def backward_half(swapped, slots_hbm, leaf_hbm, weights, sol, sep_out, leaf_out, lhs, update, sep, leaf, slots, sems):
    _, chip, core = place()
    count, size = weights.shape[0], sol.shape[-1]
    col_blocks = leaf.shape[0] // size
    row_blocks = sol.shape[1]
    cols = half_columns(1 - core if swapped else core, size)
    slots_in = pltpu.make_async_copy(slots_hbm, slots, sems.at[0])
    leaf_in = pltpu.make_async_copy(leaf_hbm.at[:, cols], leaf, sems.at[1])
    sep_back = pltpu.make_async_copy(sep, sep_out.at[:, cols], sems.at[2])
    leaf_back = pltpu.make_async_copy(leaf, leaf_out.at[:, cols], sems.at[3])
    slots_in.start()
    leaf_in.start()
    update[...] = jnp.zeros_like(update)
    rows = sep.shape[0]
    turned = sol[:, chip].reshape(size, size).T
    sep[...] = jnp.where(core == 0, turned[:rows], turned[rows:])
    sep_back.start()
    for k in range(row_blocks):
        high, low = split(sol[:, k].reshape(size, size))
        lhs[k] = jnp.concatenate([high, high, low], 1)
    slots_in.wait()

    def product(t):
        return jnp.dot(lhs[slots[t] // col_blocks], weights[t], preferred_element_type=F32)

    ahead = product(0)
    for t in range(count):
        value = ahead
        if t + 1 < count:
            ahead = product(t + 1)
        update[slots[t] % col_blocks] += value
    leaf_in.wait()
    for b in range(col_blocks):
        rows_b = slice(b * size, (b + 1) * size)
        leaf[rows_b] -= update[b].T
    leaf_back.start()
    sep_back.wait()
    leaf_back.wait()


def backward_own(slots, leaf, tiles_hbm, sol, sep_out, leaf_out, weights, tiles, tiles_sem, *rest):
    copy = pltpu.make_async_copy(tiles_hbm, tiles, tiles_sem)
    copy.start()
    copy.wait()
    for t in range(tiles.shape[0]):
        high, low = split(tiles[t])
        weights[t] = jnp.concatenate([high, low, high], 0)
    backward_half(False, slots, leaf, weights, sol, sep_out, leaf_out, *rest)


def backward_other(slots, leaf, weights, sol, sep_part, leaf_part, sep_out, leaf_out, *rest):
    backward_half(True, slots, leaf, weights, sol, sep_out, leaf_out, *rest)


def in_vmem(array):
    return pltpu.with_memory_space_constraint(array, pltpu.VMEM)


def on_device(leaf_solution, coupling, tile_slot, sep_rhs, pivot_inverse):
    n_z = lax.axis_size("z")
    n_chip = lax.axis_size("y") * lax.axis_size("x")
    slots, leaf, tiles, rhs, pivot = tile_slot[0], leaf_solution[0], coupling[0], sep_rhs, in_vmem(pivot_inverse)
    size = tiles.shape[-1]
    leaf_rows, sep_rows = leaf.shape[0], rhs.shape[0]
    col_blocks = leaf_rows // size
    vmem = pl.BlockSpec(memory_space=pltpu.VMEM)
    hbm = pl.BlockSpec(memory_space=pl.ANY)
    staging = [pltpu.VMEM(tiles.shape, F32), pltpu.SMEM(slots.shape, jnp.int32), pltpu.VMEM((leaf_rows, size), F32)]

    def forward(swapped):
        return pl.pallas_call(
            partial(forward_kernel, swapped),
            out_shape=pltpu.VMEM((n_chip, n_z, 8, size), F32),
            in_specs=[hbm, hbm, hbm, hbm],
            out_specs=vmem,
            scratch_shapes=[pltpu.VMEM((col_blocks, size, 3 * size), BF16)]
            + staging
            + [pltpu.VMEM((sep_rows, size), F32), pltpu.SemaphoreType.DMA((3 + len(CHUNKS),))],
            name="forward_send" if swapped else "forward_own",
        )(slots, leaf, tiles, rhs)

    swap = [(0, 1), (1, 0)]
    arrived = lax.ppermute(forward(True), "c", swap)
    half = forward(False) + arrived
    shared = lax.all_to_all(half, ("y", "x"), 0, 0, tiled=True)
    slab = jnp.sum(shared, 0)
    parts = lax.all_to_all(slab, "z", 0, 0, tiled=True)
    copies = pl.pallas_call(
        solve_kernel,
        out_shape=pltpu.VMEM(parts.shape, F32),
        in_specs=[vmem, vmem],
        out_specs=vmem,
        name="solve",
    )(in_vmem(parts), pivot)
    blocks = lax.all_to_all(copies, "z", 0, 0, tiled=True)
    wide = jnp.broadcast_to(blocks[None], (n_chip,) + blocks.shape)
    mine = lax.all_to_all(wide, ("y", "x"), 0, 0, tiled=True)
    other = lax.ppermute(mine, "c", swap)
    scratch = [
        pltpu.VMEM((n_z, size, 3 * size), BF16),
        pltpu.VMEM((col_blocks, size, size), F32),
        pltpu.VMEM((sep_rows, size), F32),
        pltpu.VMEM((leaf_rows, size), F32),
        pltpu.SMEM(slots.shape, jnp.int32),
        pltpu.SemaphoreType.DMA((4,)),
    ]
    results = (jax.ShapeDtypeStruct(rhs.shape, F32), jax.ShapeDtypeStruct(leaf.shape, F32))
    sep_part, leaf_part, weights = pl.pallas_call(
        backward_own,
        out_shape=results + (pltpu.VMEM((tiles.shape[0], 3 * size, size), BF16),),
        in_specs=[hbm, hbm, hbm, vmem],
        out_specs=(hbm, hbm, vmem),
        scratch_shapes=[pltpu.VMEM(tiles.shape, F32), pltpu.SemaphoreType.DMA] + scratch,
        compiler_params=pltpu.CompilerParams(vmem_limit_bytes=12 << 20),
        name="backward_own",
    )(slots, leaf, tiles, in_vmem(mine))
    sep_solution, leaf_update = pl.pallas_call(
        backward_other,
        out_shape=results,
        in_specs=[hbm, hbm, vmem, vmem, hbm, hbm],
        out_specs=(hbm, hbm),
        scratch_shapes=scratch,
        input_output_aliases={4: 0, 5: 1},
        compiler_params=pltpu.CompilerParams(vmem_limit_bytes=12 << 20),
        name="backward_other",
    )(slots, leaf, in_vmem(weights), in_vmem(other), sep_part, leaf_part)
    return sep_solution, leaf_update[None]


def solution(mesh):
    chips = mesh.devices.reshape(mesh.shape["leaf"], 4, mesh.shape["col"] // 8, 2)
    fine = Mesh(chips, ("z", "y", "x", "c"))
    col = ("y", "x", "c")
    return jax.shard_map(
        on_device,
        mesh=fine,
        in_specs=(P("z", col, None), P("z", col, None, None), P("z", col), P(col, None), P("z", None, None)),
        out_specs=(P(col, None), P("z", col, None)),
        check_vma=False,
    )
```

```python
from functools import partial

import jax
import jax.numpy as jnp
from jax import lax
from jax.experimental import pallas as pl
from jax.experimental.pallas import tpu as pltpu
from jax.sharding import PartitionSpec as P

F32 = jnp.float32
BF16 = jnp.bfloat16
CHUNKS = (8, 16)


def split(value):
    high = value.astype(BF16)
    low = (value - high.astype(F32)).astype(BF16)
    return high, low


def place():
    col = lax.axis_index("col")
    return lax.axis_index("leaf"), col // 2, col % 2


def peer_groups():
    across = [(i // 4, i % 4) for i in range(16)]
    stride = [across[3 * i % 16] for i in range(16)]
    return [[(y * 4 + x) * 2 for y, x in stride], [(x * 4 + y) * 2 + 1 for y, x in stride]]


def half_columns(core, size):
    return pl.ds(pl.multiple_of(core * size, size), size)


def start_copies(pairs, tiles_hbm, tiles, sems):
    parts = [pl.ds(sum(CHUNKS[:i]), step) for i, step in enumerate(CHUNKS)]
    pairs = pairs + [(tiles_hbm.at[part], tiles.at[part]) for part in parts]
    copies = [pltpu.make_async_copy(source, target, sems.at[i]) for i, (source, target) in enumerate(pairs)]
    for copy in copies:
        copy.start()
    return copies[: -len(CHUNKS)], copies[-len(CHUNKS) :]


def pipelined(copies, count, product, use):
    first = {sum(CHUNKS[:i]): copy for i, copy in enumerate(copies)}
    ahead = None
    for t in range(count + 1):
        value = ahead
        if t < count:
            if t in first:
                first[t].wait()
            ahead = product(t)
        if t > 0:
            use(t - 1, value)


def forward_kernel(swapped, slots_hbm, leaf_hbm, tiles_hbm, rhs_hbm, out, lhs, tiles, slots, leaf, rhs, sems):
    z, chip, core = place()
    count, size = tiles.shape[0], tiles.shape[1]
    col_blocks = leaf.shape[0] // size
    slabs = out.shape[0]
    cols = half_columns(1 - core if swapped else core, size)
    small, copies = start_copies(
        [(leaf_hbm.at[:, cols], leaf), (slots_hbm, slots), (rhs_hbm.at[:, cols], rhs)], tiles_hbm, tiles, sems
    )
    out[...] = jnp.zeros_like(out)
    small[0].wait()
    for b in range(col_blocks):
        high, low = split(leaf[b * size : (b + 1) * size].T)
        lhs[b] = jnp.concatenate([high, high, low], 1)
    small[1].wait()
    small[2].wait()
    lane = lax.broadcasted_iota(jnp.int32, (size, size), 1)
    keep = (lane // (size // 2) == core) & (z == 0)
    placed = jnp.where(keep, jnp.concatenate([rhs[...], rhs[...]], 0).T, 0.0)
    out[:, chip] = placed.reshape(slabs, 8, size)

    def product(t):
        high, low = split(tiles[t])
        weights = jnp.concatenate([high.T, low.T, high.T], 0)
        return jnp.dot(lhs[slots[t] % col_blocks], weights, preferred_element_type=F32)

    def use(t, value):
        out[:, slots[t] // col_blocks] -= value.reshape(slabs, 8, size)

    pipelined(copies, count, product, use)


def solve_kernel(parts, pivot, out):
    total = jnp.sum(parts[...], 0)
    solved = jnp.dot(total, pivot[0], preferred_element_type=F32, precision=lax.Precision.HIGHEST)
    out[...] = jnp.broadcast_to(solved[None], out.shape)


def backward_half(swapped, slots_hbm, leaf_hbm, weights, sol, sep_out, leaf_out, lhs, update, sep, leaf, slots, sems):
    _, chip, core = place()
    count, size = weights.shape[0], sol.shape[-1]
    col_blocks = leaf.shape[0] // size
    row_blocks = sol.shape[1]
    cols = half_columns(1 - core if swapped else core, size)
    slots_in = pltpu.make_async_copy(slots_hbm, slots, sems.at[0])
    leaf_in = pltpu.make_async_copy(leaf_hbm.at[:, cols], leaf, sems.at[1])
    sep_back = pltpu.make_async_copy(sep, sep_out.at[:, cols], sems.at[2])
    leaf_back = pltpu.make_async_copy(leaf, leaf_out.at[:, cols], sems.at[3])
    slots_in.start()
    leaf_in.start()
    update[...] = jnp.zeros_like(update)
    rows = sep.shape[0]
    turned = sol[:, chip].reshape(size, size).T
    sep[...] = jnp.where(core == 0, turned[:rows], turned[rows:])
    sep_back.start()
    for k in range(row_blocks):
        high, low = split(sol[:, k].reshape(size, size))
        lhs[k] = jnp.concatenate([high, high, low], 1)
    slots_in.wait()

    def product(t):
        return jnp.dot(lhs[slots[t] // col_blocks], weights[t], preferred_element_type=F32)

    ahead = product(0)
    for t in range(count):
        value = ahead
        if t + 1 < count:
            ahead = product(t + 1)
        update[slots[t] % col_blocks] += value
    leaf_in.wait()
    for b in range(col_blocks):
        rows_b = slice(b * size, (b + 1) * size)
        leaf[rows_b] -= update[b].T
    leaf_back.start()
    sep_back.wait()
    leaf_back.wait()


def backward_own(slots, leaf, tiles_hbm, sol, sep_out, leaf_out, weights, tiles, tiles_sem, *rest):
    copy = pltpu.make_async_copy(tiles_hbm, tiles, tiles_sem)
    copy.start()
    copy.wait()
    for t in range(tiles.shape[0]):
        high, low = split(tiles[t])
        weights[t] = jnp.concatenate([high, low, high], 0)
    backward_half(False, slots, leaf, weights, sol, sep_out, leaf_out, *rest)


def backward_other(slots, leaf, weights, sol, sep_part, leaf_part, sep_out, leaf_out, *rest):
    backward_half(True, slots, leaf, weights, sol, sep_out, leaf_out, *rest)


def in_vmem(array):
    return pltpu.with_memory_space_constraint(array, pltpu.VMEM)


def on_device(leaf_solution, coupling, tile_slot, sep_rhs, pivot_inverse):
    n_z = lax.axis_size("leaf")
    n_chip = lax.axis_size("col") // 2
    groups = peer_groups()
    slots, leaf, tiles, rhs, pivot = tile_slot[0], leaf_solution[0], coupling[0], sep_rhs, in_vmem(pivot_inverse)
    size = tiles.shape[-1]
    leaf_rows, sep_rows = leaf.shape[0], rhs.shape[0]
    col_blocks = leaf_rows // size
    vmem = pl.BlockSpec(memory_space=pltpu.VMEM)
    hbm = pl.BlockSpec(memory_space=pl.ANY)
    staging = [pltpu.VMEM(tiles.shape, F32), pltpu.SMEM(slots.shape, jnp.int32), pltpu.VMEM((leaf_rows, size), F32)]

    def forward(swapped):
        return pl.pallas_call(
            partial(forward_kernel, swapped),
            out_shape=pltpu.VMEM((n_chip, n_z, 8, size), F32),
            in_specs=[hbm, hbm, hbm, hbm],
            out_specs=vmem,
            scratch_shapes=[pltpu.VMEM((col_blocks, size, 3 * size), BF16)]
            + staging
            + [pltpu.VMEM((sep_rows, size), F32), pltpu.SemaphoreType.DMA((3 + len(CHUNKS),))],
            name="forward_send" if swapped else "forward_own",
        )(slots, leaf, tiles, rhs)

    swap = [(i, i ^ 1) for i in range(2 * n_chip)]
    arrived = lax.ppermute(forward(True), "col", swap)
    half = forward(False) + arrived
    shared = lax.all_to_all(half, "col", 0, 0, axis_index_groups=groups, tiled=True)
    slab = jnp.sum(shared, 0)
    parts = lax.all_to_all(slab, "leaf", 0, 0, tiled=True)
    copies = pl.pallas_call(
        solve_kernel,
        out_shape=pltpu.VMEM(parts.shape, F32),
        in_specs=[vmem, vmem],
        out_specs=vmem,
        name="solve",
    )(in_vmem(parts), pivot)
    blocks = lax.all_to_all(copies, "leaf", 0, 0, tiled=True)
    wide = jnp.broadcast_to(blocks[None], (n_chip,) + blocks.shape)
    mine = lax.all_to_all(wide, "col", 0, 0, axis_index_groups=groups, tiled=True)
    other = lax.ppermute(mine, "col", swap)
    scratch = [
        pltpu.VMEM((n_z, size, 3 * size), BF16),
        pltpu.VMEM((col_blocks, size, size), F32),
        pltpu.VMEM((sep_rows, size), F32),
        pltpu.VMEM((leaf_rows, size), F32),
        pltpu.SMEM(slots.shape, jnp.int32),
        pltpu.SemaphoreType.DMA((4,)),
    ]
    results = (jax.ShapeDtypeStruct(rhs.shape, F32), jax.ShapeDtypeStruct(leaf.shape, F32))
    sep_part, leaf_part, weights = pl.pallas_call(
        backward_own,
        out_shape=results + (pltpu.VMEM((tiles.shape[0], 3 * size, size), BF16),),
        in_specs=[hbm, hbm, hbm, vmem],
        out_specs=(hbm, hbm, vmem),
        scratch_shapes=[pltpu.VMEM(tiles.shape, F32), pltpu.SemaphoreType.DMA] + scratch,
        compiler_params=pltpu.CompilerParams(vmem_limit_bytes=12 << 20),
        name="backward_own",
    )(slots, leaf, tiles, in_vmem(mine))
    sep_solution, leaf_update = pl.pallas_call(
        backward_other,
        out_shape=results,
        in_specs=[hbm, hbm, vmem, vmem, hbm, hbm],
        out_specs=(hbm, hbm),
        scratch_shapes=scratch,
        input_output_aliases={4: 0, 5: 1},
        compiler_params=pltpu.CompilerParams(vmem_limit_bytes=12 << 20),
        name="backward_other",
    )(slots, leaf, in_vmem(weights), in_vmem(other), sep_part, leaf_part)
    return sep_solution, leaf_update[None]


def solution(mesh):
    return jax.shard_map(
        on_device,
        mesh=mesh,
        in_specs=(
            P("leaf", "col", None),
            P("leaf", "col", None, None),
            P("leaf", "col"),
            P("col", None),
            P("leaf", None, None),
        ),
        out_specs=(P("col", None), P("leaf", "col", None)),
        check_vma=False,
    )
```

```python
from functools import partial

import jax
import jax.numpy as jnp
from jax import lax
from jax.experimental import pallas as pl
from jax.experimental.pallas import tpu as pltpu
from jax.sharding import PartitionSpec as P

F32 = jnp.float32
BF16 = jnp.bfloat16
CHUNKS = (8, 16)


def split(value):
    high = value.astype(BF16)
    low = (value - high.astype(F32)).astype(BF16)
    return high, low


def place():
    col = lax.axis_index("col")
    return lax.axis_index("leaf"), col // 2, col % 2


def plane_groups():
    chips = [((i // 4 + 2) % 4) * 4 + (i + 2) % 4 for i in range(16)]
    turned = [chip % 4 * 4 + chip // 4 for chip in chips]
    return [[2 * chip for chip in chips], [2 * chip + 1 for chip in turned]]


def half_columns(core, size):
    return pl.ds(pl.multiple_of(core * size, size), size)


def start_copies(pairs, tiles_hbm, tiles, sems):
    parts = [pl.ds(sum(CHUNKS[:i]), step) for i, step in enumerate(CHUNKS)]
    pairs = pairs + [(tiles_hbm.at[part], tiles.at[part]) for part in parts]
    copies = [pltpu.make_async_copy(source, target, sems.at[i]) for i, (source, target) in enumerate(pairs)]
    for copy in copies:
        copy.start()
    return copies[: -len(CHUNKS)], copies[-len(CHUNKS) :]


def pipelined(copies, count, product, use):
    first = {sum(CHUNKS[:i]): copy for i, copy in enumerate(copies)}
    ahead = None
    for t in range(count + 1):
        value = ahead
        if t < count:
            if t in first:
                first[t].wait()
            ahead = product(t)
        if t > 0:
            use(t - 1, value)


def forward_kernel(swapped, slots_hbm, leaf_hbm, tiles_hbm, rhs_hbm, out, lhs, tiles, slots, leaf, rhs, sems):
    z, chip, core = place()
    count, size = tiles.shape[0], tiles.shape[1]
    col_blocks = leaf.shape[0] // size
    slabs = out.shape[0]
    cols = half_columns(1 - core if swapped else core, size)
    small, copies = start_copies(
        [(leaf_hbm.at[:, cols], leaf), (slots_hbm, slots), (rhs_hbm.at[:, cols], rhs)], tiles_hbm, tiles, sems
    )
    out[...] = jnp.zeros_like(out)
    small[0].wait()
    for b in range(col_blocks):
        high, low = split(leaf[b * size : (b + 1) * size].T)
        lhs[b] = jnp.concatenate([high, high, low], 1)
    small[1].wait()
    small[2].wait()
    lane = lax.broadcasted_iota(jnp.int32, (size, size), 1)
    keep = (lane // (size // 2) == core) & (z == 0)
    placed = jnp.where(keep, jnp.concatenate([rhs[...], rhs[...]], 0).T, 0.0)
    out[:, chip] = placed.reshape(slabs, 8, size)

    def product(t):
        high, low = split(tiles[t])
        weights = jnp.concatenate([high.T, low.T, high.T], 0)
        return jnp.dot(lhs[slots[t] % col_blocks], weights, preferred_element_type=F32)

    def use(t, value):
        out[:, slots[t] // col_blocks] -= value.reshape(slabs, 8, size)

    pipelined(copies, count, product, use)


def solve_kernel(parts, pivot, out):
    total = jnp.sum(parts[...], 0)
    solved = jnp.dot(total, pivot[0], preferred_element_type=F32, precision=lax.Precision.HIGHEST)
    out[...] = jnp.broadcast_to(solved[None], out.shape)


def backward_half(swapped, slots_hbm, leaf_hbm, weights, sol, sep_out, leaf_out, lhs, update, sep, leaf, slots, sems):
    _, chip, core = place()
    count, size = weights.shape[0], sol.shape[-1]
    col_blocks = leaf.shape[0] // size
    row_blocks = sol.shape[1]
    cols = half_columns(1 - core if swapped else core, size)
    slots_in = pltpu.make_async_copy(slots_hbm, slots, sems.at[0])
    leaf_in = pltpu.make_async_copy(leaf_hbm.at[:, cols], leaf, sems.at[1])
    sep_back = pltpu.make_async_copy(sep, sep_out.at[:, cols], sems.at[2])
    leaf_back = pltpu.make_async_copy(leaf, leaf_out.at[:, cols], sems.at[3])
    slots_in.start()
    leaf_in.start()
    update[...] = jnp.zeros_like(update)
    rows = sep.shape[0]
    turned = sol[:, chip].reshape(size, size).T
    sep[...] = jnp.where(core == 0, turned[:rows], turned[rows:])
    sep_back.start()
    for k in range(row_blocks):
        high, low = split(sol[:, k].reshape(size, size))
        lhs[k] = jnp.concatenate([high, high, low], 1)
    slots_in.wait()

    def product(t):
        return jnp.dot(lhs[slots[t] // col_blocks], weights[t], preferred_element_type=F32)

    ahead = product(0)
    for t in range(count):
        value = ahead
        if t + 1 < count:
            ahead = product(t + 1)
        update[slots[t] % col_blocks] += value
    leaf_in.wait()
    for b in range(col_blocks):
        rows_b = slice(b * size, (b + 1) * size)
        leaf[rows_b] -= update[b].T
    leaf_back.start()
    sep_back.wait()
    leaf_back.wait()


def backward_own(slots, leaf, tiles_hbm, sol, sep_out, leaf_out, weights, tiles, tiles_sem, *rest):
    copy = pltpu.make_async_copy(tiles_hbm, tiles, tiles_sem)
    copy.start()
    copy.wait()
    for t in range(tiles.shape[0]):
        high, low = split(tiles[t])
        weights[t] = jnp.concatenate([high, low, high], 0)
    backward_half(False, slots, leaf, weights, sol, sep_out, leaf_out, *rest)


def backward_other(slots, leaf, weights, sol, sep_part, leaf_part, sep_out, leaf_out, *rest):
    backward_half(True, slots, leaf, weights, sol, sep_out, leaf_out, *rest)


def in_vmem(array):
    return pltpu.with_memory_space_constraint(array, pltpu.VMEM)


def on_device(leaf_solution, coupling, tile_slot, sep_rhs, pivot_inverse):
    n_z = lax.axis_size("leaf")
    n_chip = lax.axis_size("col") // 2
    groups = plane_groups()
    slots, leaf, tiles, rhs, pivot = tile_slot[0], leaf_solution[0], coupling[0], sep_rhs, in_vmem(pivot_inverse)
    size = tiles.shape[-1]
    leaf_rows, sep_rows = leaf.shape[0], rhs.shape[0]
    col_blocks = leaf_rows // size
    vmem = pl.BlockSpec(memory_space=pltpu.VMEM)
    hbm = pl.BlockSpec(memory_space=pl.ANY)
    staging = [pltpu.VMEM(tiles.shape, F32), pltpu.SMEM(slots.shape, jnp.int32), pltpu.VMEM((leaf_rows, size), F32)]

    def forward(swapped):
        return pl.pallas_call(
            partial(forward_kernel, swapped),
            out_shape=pltpu.VMEM((n_chip, n_z, 8, size), F32),
            in_specs=[hbm, hbm, hbm, hbm],
            out_specs=vmem,
            scratch_shapes=[pltpu.VMEM((col_blocks, size, 3 * size), BF16)]
            + staging
            + [pltpu.VMEM((sep_rows, size), F32), pltpu.SemaphoreType.DMA((3 + len(CHUNKS),))],
            name="forward_send" if swapped else "forward_own",
        )(slots, leaf, tiles, rhs)

    swap = [(i, i ^ 1) for i in range(2 * n_chip)]
    arrived = lax.ppermute(forward(True), "col", swap)
    half = forward(False) + arrived
    shared = lax.all_to_all(half, "col", 0, 0, axis_index_groups=groups, tiled=True)
    slab = jnp.sum(shared, 0)
    parts = lax.all_to_all(slab, "leaf", 0, 0, tiled=True)
    copies = pl.pallas_call(
        solve_kernel,
        out_shape=pltpu.VMEM(parts.shape, F32),
        in_specs=[vmem, vmem],
        out_specs=vmem,
        name="solve",
    )(in_vmem(parts), pivot)
    blocks = lax.all_to_all(copies, "leaf", 0, 0, tiled=True)
    wide = jnp.broadcast_to(blocks[None], (n_chip,) + blocks.shape)
    mine = lax.all_to_all(wide, "col", 0, 0, axis_index_groups=groups, tiled=True)
    other = lax.ppermute(mine, "col", swap)
    scratch = [
        pltpu.VMEM((n_z, size, 3 * size), BF16),
        pltpu.VMEM((col_blocks, size, size), F32),
        pltpu.VMEM((sep_rows, size), F32),
        pltpu.VMEM((leaf_rows, size), F32),
        pltpu.SMEM(slots.shape, jnp.int32),
        pltpu.SemaphoreType.DMA((4,)),
    ]
    results = (jax.ShapeDtypeStruct(rhs.shape, F32), jax.ShapeDtypeStruct(leaf.shape, F32))
    sep_part, leaf_part, weights = pl.pallas_call(
        backward_own,
        out_shape=results + (pltpu.VMEM((tiles.shape[0], 3 * size, size), BF16),),
        in_specs=[hbm, hbm, hbm, vmem],
        out_specs=(hbm, hbm, vmem),
        scratch_shapes=[pltpu.VMEM(tiles.shape, F32), pltpu.SemaphoreType.DMA] + scratch,
        compiler_params=pltpu.CompilerParams(vmem_limit_bytes=12 << 20),
        name="backward_own",
    )(slots, leaf, tiles, in_vmem(mine))
    sep_solution, leaf_update = pl.pallas_call(
        backward_other,
        out_shape=results,
        in_specs=[hbm, hbm, vmem, vmem, hbm, hbm],
        out_specs=(hbm, hbm),
        scratch_shapes=scratch,
        input_output_aliases={4: 0, 5: 1},
        compiler_params=pltpu.CompilerParams(vmem_limit_bytes=12 << 20),
        name="backward_other",
    )(slots, leaf, in_vmem(weights), in_vmem(other), sep_part, leaf_part)
    return sep_solution, leaf_update[None]


def solution(mesh):
    return jax.shard_map(
        on_device,
        mesh=mesh,
        in_specs=(
            P("leaf", "col", None),
            P("leaf", "col", None, None),
            P("leaf", "col"),
            P("col", None),
            P("leaf", None, None),
        ),
        out_specs=(P("col", None), P("leaf", "col", None)),
        check_vma=False,
    )
```

```python
from functools import partial

import jax
import jax.numpy as jnp
from jax import lax
from jax.experimental import pallas as pl
from jax.experimental.pallas import tpu as pltpu
from jax.sharding import PartitionSpec as P

F32 = jnp.float32
BF16 = jnp.bfloat16
CHUNKS = (8, 16)
FIRST = 10


def split(value):
    high = value.astype(BF16)
    low = (value - high.astype(F32)).astype(BF16)
    return high, low


def place():
    col = lax.axis_index("col")
    return lax.axis_index("leaf"), col // 2, col % 2


def plane_groups():
    chips = [((i // 4 + 2) % 4) * 4 + (i + 2) % 4 for i in range(16)]
    turned = [chip % 4 * 4 + chip // 4 for chip in chips]
    return [[2 * chip for chip in chips], [2 * chip + 1 for chip in turned]]


def slot_of(block, count):
    return (block + count - FIRST) % count


def half_columns(core, size):
    return pl.ds(pl.multiple_of(core * size, size), size)


def start_copies(pairs, tiles_hbm, tiles, sems):
    parts = [pl.ds(sum(CHUNKS[:i]), step) for i, step in enumerate(CHUNKS)]
    pairs = pairs + [(tiles_hbm.at[part], tiles.at[part]) for part in parts]
    copies = [pltpu.make_async_copy(source, target, sems.at[i]) for i, (source, target) in enumerate(pairs)]
    for copy in copies:
        copy.start()
    return copies[: -len(CHUNKS)], copies[-len(CHUNKS) :]


def pipelined(copies, count, product, use):
    first = {sum(CHUNKS[:i]): copy for i, copy in enumerate(copies)}
    ahead = None
    for t in range(count + 1):
        value = ahead
        if t < count:
            if t in first:
                first[t].wait()
            ahead = product(t)
        if t > 0:
            use(t - 1, value)


def forward_kernel(swapped, slots_hbm, leaf_hbm, tiles_hbm, rhs_hbm, out, lhs, tiles, slots, leaf, rhs, sems):
    z, chip, core = place()
    count, size = tiles.shape[0], tiles.shape[1]
    col_blocks = leaf.shape[0] // size
    slabs, row_blocks = out.shape[0], out.shape[1]
    cols = half_columns(1 - core if swapped else core, size)
    small, copies = start_copies(
        [(leaf_hbm.at[:, cols], leaf), (slots_hbm, slots), (rhs_hbm.at[:, cols], rhs)], tiles_hbm, tiles, sems
    )
    out[...] = jnp.zeros_like(out)
    small[0].wait()
    for b in range(col_blocks):
        high, low = split(leaf[b * size : (b + 1) * size].T)
        lhs[b] = jnp.concatenate([high, high, low], 1)
    small[1].wait()
    small[2].wait()
    lane = lax.broadcasted_iota(jnp.int32, (size, size), 1)
    keep = (lane // (size // 2) == core) & (z == 0)
    placed = jnp.where(keep, jnp.concatenate([rhs[...], rhs[...]], 0).T, 0.0)
    out[:, slot_of(chip, row_blocks)] = placed.reshape(slabs, 8, size)

    def product(t):
        high, low = split(tiles[t])
        weights = jnp.concatenate([high.T, low.T, high.T], 0)
        return jnp.dot(lhs[slots[t] % col_blocks], weights, preferred_element_type=F32)

    def use(t, value):
        out[:, slot_of(slots[t] // col_blocks, row_blocks)] -= value.reshape(slabs, 8, size)

    pipelined(copies, count, product, use)


def solve_kernel(parts, pivot, out):
    total = jnp.sum(parts[...], 0)
    solved = jnp.dot(total, pivot[0], preferred_element_type=F32, precision=lax.Precision.HIGHEST)
    out[...] = jnp.broadcast_to(solved[None], out.shape)


def backward_half(swapped, slots_hbm, leaf_hbm, weights, sol, sep_out, leaf_out, lhs, update, sep, leaf, slots, sems):
    _, chip, core = place()
    count, size = weights.shape[0], sol.shape[-1]
    col_blocks = leaf.shape[0] // size
    row_blocks = sol.shape[1]
    cols = half_columns(1 - core if swapped else core, size)
    slots_in = pltpu.make_async_copy(slots_hbm, slots, sems.at[0])
    leaf_in = pltpu.make_async_copy(leaf_hbm.at[:, cols], leaf, sems.at[1])
    sep_back = pltpu.make_async_copy(sep, sep_out.at[:, cols], sems.at[2])
    leaf_back = pltpu.make_async_copy(leaf, leaf_out.at[:, cols], sems.at[3])
    slots_in.start()
    leaf_in.start()
    update[...] = jnp.zeros_like(update)
    rows = sep.shape[0]
    turned = sol[:, slot_of(chip, row_blocks)].reshape(size, size).T
    sep[...] = jnp.where(core == 0, turned[:rows], turned[rows:])
    sep_back.start()
    for k in range(row_blocks):
        high, low = split(sol[:, k].reshape(size, size))
        lhs[k] = jnp.concatenate([high, high, low], 1)
    slots_in.wait()

    def product(t):
        return jnp.dot(lhs[slot_of(slots[t] // col_blocks, row_blocks)], weights[t], preferred_element_type=F32)

    ahead = product(0)
    for t in range(count):
        value = ahead
        if t + 1 < count:
            ahead = product(t + 1)
        update[slots[t] % col_blocks] += value
    leaf_in.wait()
    for b in range(col_blocks):
        rows_b = slice(b * size, (b + 1) * size)
        leaf[rows_b] -= update[b].T
    leaf_back.start()
    sep_back.wait()
    leaf_back.wait()


def backward_own(slots, leaf, tiles_hbm, sol, sep_out, leaf_out, weights, tiles, tiles_sem, *rest):
    copy = pltpu.make_async_copy(tiles_hbm, tiles, tiles_sem)
    copy.start()
    copy.wait()
    for t in range(tiles.shape[0]):
        high, low = split(tiles[t])
        weights[t] = jnp.concatenate([high, low, high], 0)
    backward_half(False, slots, leaf, weights, sol, sep_out, leaf_out, *rest)


def backward_other(slots, leaf, weights, sol, sep_part, leaf_part, sep_out, leaf_out, *rest):
    backward_half(True, slots, leaf, weights, sol, sep_out, leaf_out, *rest)


def in_vmem(array):
    return pltpu.with_memory_space_constraint(array, pltpu.VMEM)


def on_device(leaf_solution, coupling, tile_slot, sep_rhs, pivot_inverse):
    n_z = lax.axis_size("leaf")
    n_chip = lax.axis_size("col") // 2
    groups = plane_groups()
    ring = [[(FIRST + i) % n_z for i in range(n_z)]]
    slots, leaf, tiles, rhs, pivot = tile_slot[0], leaf_solution[0], coupling[0], sep_rhs, in_vmem(pivot_inverse)
    size = tiles.shape[-1]
    leaf_rows, sep_rows = leaf.shape[0], rhs.shape[0]
    col_blocks = leaf_rows // size
    vmem = pl.BlockSpec(memory_space=pltpu.VMEM)
    hbm = pl.BlockSpec(memory_space=pl.ANY)
    staging = [pltpu.VMEM(tiles.shape, F32), pltpu.SMEM(slots.shape, jnp.int32), pltpu.VMEM((leaf_rows, size), F32)]

    def forward(swapped):
        return pl.pallas_call(
            partial(forward_kernel, swapped),
            out_shape=pltpu.VMEM((n_chip, n_z, 8, size), F32),
            in_specs=[hbm, hbm, hbm, hbm],
            out_specs=vmem,
            scratch_shapes=[pltpu.VMEM((col_blocks, size, 3 * size), BF16)]
            + staging
            + [pltpu.VMEM((sep_rows, size), F32), pltpu.SemaphoreType.DMA((3 + len(CHUNKS),))],
            name="forward_send" if swapped else "forward_own",
        )(slots, leaf, tiles, rhs)

    swap = [(i, i ^ 1) for i in range(2 * n_chip)]
    arrived = lax.ppermute(forward(True), "col", swap)
    half = forward(False) + arrived
    shared = lax.all_to_all(half, "col", 0, 0, axis_index_groups=groups, tiled=True)
    slab = jnp.sum(shared, 0)
    parts = lax.all_to_all(slab, "leaf", 0, 0, axis_index_groups=ring, tiled=True)
    copies = pl.pallas_call(
        solve_kernel,
        out_shape=pltpu.VMEM(parts.shape, F32),
        in_specs=[vmem, vmem],
        out_specs=vmem,
        name="solve",
    )(in_vmem(parts), pivot)
    blocks = lax.all_to_all(copies, "leaf", 0, 0, axis_index_groups=ring, tiled=True)
    wide = jnp.broadcast_to(blocks[None], (n_chip,) + blocks.shape)
    mine = lax.all_to_all(wide, "col", 0, 0, axis_index_groups=groups, tiled=True)
    other = lax.ppermute(mine, "col", swap)
    scratch = [
        pltpu.VMEM((n_z, size, 3 * size), BF16),
        pltpu.VMEM((col_blocks, size, size), F32),
        pltpu.VMEM((sep_rows, size), F32),
        pltpu.VMEM((leaf_rows, size), F32),
        pltpu.SMEM(slots.shape, jnp.int32),
        pltpu.SemaphoreType.DMA((4,)),
    ]
    results = (jax.ShapeDtypeStruct(rhs.shape, F32), jax.ShapeDtypeStruct(leaf.shape, F32))
    sep_part, leaf_part, weights = pl.pallas_call(
        backward_own,
        out_shape=results + (pltpu.VMEM((tiles.shape[0], 3 * size, size), BF16),),
        in_specs=[hbm, hbm, hbm, vmem],
        out_specs=(hbm, hbm, vmem),
        scratch_shapes=[pltpu.VMEM(tiles.shape, F32), pltpu.SemaphoreType.DMA] + scratch,
        compiler_params=pltpu.CompilerParams(vmem_limit_bytes=12 << 20),
        name="backward_own",
    )(slots, leaf, tiles, in_vmem(mine))
    sep_solution, leaf_update = pl.pallas_call(
        backward_other,
        out_shape=results,
        in_specs=[hbm, hbm, vmem, vmem, hbm, hbm],
        out_specs=(hbm, hbm),
        scratch_shapes=scratch,
        input_output_aliases={4: 0, 5: 1},
        compiler_params=pltpu.CompilerParams(vmem_limit_bytes=12 << 20),
        name="backward_other",
    )(slots, leaf, in_vmem(weights), in_vmem(other), sep_part, leaf_part)
    return sep_solution, leaf_update[None]


def solution(mesh):
    return jax.shard_map(
        on_device,
        mesh=mesh,
        in_specs=(
            P("leaf", "col", None),
            P("leaf", "col", None, None),
            P("leaf", "col"),
            P("col", None),
            P("leaf", None, None),
        ),
        out_specs=(P("col", None), P("leaf", "col", None)),
        check_vma=False,
    )
```
